256 devices in a mesh: elem: 16 (over y, z_hi), grp: 16 (over z_lo, x, core).
Axes of the slice: x: 4, y: 4, z: 8 (z_hi: 4, z_lo: 2; z = z_hi * 2 + z_lo), core: 2. Of those that a mesh axis runs over, the one named last changes fastest.
Arguments:
- basis_values: bfloat16 [16, 1024, 32768], P('elem', 'grp'), may hold values from -0.03125 to 0.03125
- basis_derivs: bfloat16 [16, 1024, 32768], P('elem', 'grp'), may hold values from -0.03125 to 0.03125
- potential: float32 [16, 32768], P('elem', 'grp'), may hold values from 0.5 to 2
- hop_blocks: bfloat16 [16, 4, 1024, 1024], P('elem', None, 'grp'), may hold values from -0.1875 to 0.1875
- coeffs: bfloat16 [16, 1024, 4096], P('elem', None, 'grp'), may hold values from -6 to 6
- counts: int32 [16], replicated, may hold values from 256 to 1024, as said below
- neighbours: int32 [16, 4], replicated, may hold values from 0 to 15, as said below
Outputs:
- applied_bands: float32 [16, 1024, 4096], P('elem', None, 'grp')
The draws below stay inside these ranges and needn't reach their ends.
Inputs may be any that keep to these rules, and one draw needn't show every extreme that they name: `counts`: count of live basis functions of each element; some element has exactly 1024 and some exactly 256. `neighbours`: four distinct elements, none the element itself.
All inputs are finite; a program needn't handle non-finite values.
Results may differ from the reference program's by a relative error of at most 0.0022.
Values may be sent and summed in bfloat16 or wider, within the bound.
No kernel may reach another device: no remote copies, remote signals or barrier semaphores. Data moves between devices by JAX's collectives and lax.ppermute only.
A program may use at most 192 MiB of HBM per device.

```python
import jax
import jax.numpy as jnp
from jax import lax

MAXB = 1024
BANDS = 4096
NEIGH = 4
P_SIZE = 32768
NELEM = 16


def draw_counts(key, part):
    first_key, second_key = jax.random.split(key)
    raw_counts = jax.random.randint(first_key, (NELEM,), MAXB // 4, MAXB + 1)
    spots = jax.random.permutation(second_key, NELEM)
    raw_counts = raw_counts.at[spots[0]].set(MAXB).at[spots[1]].set(MAXB // 4)
    return raw_counts.astype(jnp.int32)


def draw_neighbours(key, part):
    chain_order = jax.random.permutation(key, NELEM).astype(jnp.int32)
    places = jnp.argsort(chain_order, stable=True).astype(jnp.int32)
    offsets = jnp.array([-2, -1, 1, 2], dtype=jnp.int32)
    return chain_order[(places[:, None] + offsets[None, :]) % NELEM].astype(jnp.int32)


def block_scale(rng, dims, pieces, least, top_value):
    def one(position, blocks):
        draws = jax.random.uniform(jax.random.fold_in(jax.random.fold_in(rng, 6), position), (blocks,), jnp.float32, least / len(pieces), top_value / len(pieces))
        return jnp.repeat(jnp.exp(draws), dims[position] // blocks).reshape((-1,) + (1,) * (len(dims) - position - 1))

    gain = one(*pieces[0])
    for cut in pieces[1:]:
        gain = gain * one(*cut)
    return gain


def scatter_about(rng, dims, spread, reach, pieces=(), kind=jnp.bfloat16):
    drawn = spread * jax.random.normal(rng, dims, jnp.float32)
    if pieces:
        drawn = drawn * block_scale(rng, dims, pieces, -0.22, 0.18)
    return jnp.clip(drawn, -reach, reach).astype(kind)


def setup_inputs(seed: int = 0) -> dict:
    streams_of = jax.random.split(jax.random.key(seed), 8)
    return {
        "basis_values": scatter_about(streams_of[0], (NELEM, MAXB, P_SIZE), P_SIZE ** -0.5, 0.03125, ((0, 16), (1, 16))),
        "basis_derivs": scatter_about(streams_of[1], (NELEM, MAXB, P_SIZE), P_SIZE ** -0.5, 0.03125, ((0, 16), (1, 16))),
        "potential": jnp.clip(0.5 + 1.5 * jax.random.uniform(streams_of[2], (NELEM, P_SIZE), jnp.float32) ** block_scale(streams_of[2], (NELEM, P_SIZE), ((0, 16), (1, 16)), -0.2, 0.2), 0.5, 2.0),
        "hop_blocks": scatter_about(streams_of[3], (NELEM, NEIGH, MAXB, MAXB), MAXB ** -0.5, 0.1875, ((0, 16), (2, 16))),
        "coeffs": scatter_about(streams_of[4], (NELEM, MAXB, BANDS), 1.0, 6.0, ((0, 16), (2, 16))),
        "counts": draw_counts(jax.random.fold_in(streams_of[7], 71), 0),
        "neighbours": draw_neighbours(jax.random.fold_in(streams_of[7], 71), 0),
    }


def reference(basis_values, basis_derivs, potential, hop_blocks, coeffs, counts, neighbours):
    row_ids = jnp.arange(MAXB, dtype=jnp.int32)
    live_rows = row_ids[None, :] < counts[:, None]
    masked = jnp.where(live_rows[:, :, None], coeffs, jnp.zeros_like(coeffs))

    def element_term(element):
        values_here = basis_values[element]
        derivs_here = basis_derivs[element]
        weighted = (potential[element][None, :] * values_here.astype(jnp.float32)).astype(jnp.bfloat16)
        assembled = 0.5 * jnp.dot(derivs_here, derivs_here.T, preferred_element_type=jnp.float32)
        assembled = assembled + jnp.dot(values_here, weighted.T, preferred_element_type=jnp.float32)
        assembled_low = assembled.astype(jnp.bfloat16)
        applied = jnp.dot(assembled_low, masked[element], preferred_element_type=jnp.float32)
        for which in range(NEIGH):
            applied = applied + jnp.dot(hop_blocks[element, which], masked[neighbours[element, which]], preferred_element_type=jnp.float32)
        return jnp.where(live_rows[element][:, None], applied, jnp.zeros_like(applied))

    return lax.map(element_term, jnp.arange(NELEM, dtype=jnp.int32))
```

```python
import jax
import jax.numpy as jnp
from jax import lax
from jax.experimental import pallas as pl
from jax.experimental.pallas import tpu as pltpu
from jax.sharding import Mesh, PartitionSpec as P

ELEM = ("y", "zh")
CHIPS = ("zl", "x")
GRP = ("zl", "x", "c")
CORES = 2


def swap_cores(a):
    return lax.ppermute(a, "c", [(0, 1), (1, 0)])


def spread(a):
    chips = lax.axis_size(CHIPS)
    return lax.all_to_all(
        jnp.broadcast_to(a[None], (chips, *a.shape)), CHIPS, 0, 0, tiled=True
    )


def slab(a):
    rows, points = a.shape
    devices = lax.axis_size(GRP)
    a = a.reshape(rows, devices, points // devices).transpose(1, 0, 2)
    a = lax.all_to_all(a, GRP, 0, 0, tiled=True)
    return a.reshape(devices * rows, points // devices)


def masked_copy(dst, src, count):
    rows = lax.broadcasted_iota(jnp.int32, src.shape, 0)
    src = src.astype(jnp.float32)
    dst[...] = jnp.where(rows < count, src, jnp.zeros_like(src)).astype(dst.dtype)


def hop_kernel(pos, counts, near, mine_ref, other_ref, *refs):
    x_refs, o_ref, masked = refs[:-2], refs[-2], refs[-1]
    step, k = pl.program_id(0), pl.program_id(1)
    width = masked.shape[1]

    @pl.when(step == 0)
    def _():
        for i, x_ref in enumerate(x_refs):

            @pl.when(k == i)
            def _():
                masked_copy(masked.at[i], x_ref[0], counts[near[pos[1], i]])

    def add(a_ref):
        lhs = a_ref[:, 0].reshape(-1, width)
        part = jnp.dot(lhs, masked[k], preferred_element_type=jnp.float32)
        part = part.reshape(o_ref.shape)

        @pl.when(k == 0)
        def _():
            o_ref[...] = part

        @pl.when(k > 0)
        def _():
            o_ref[...] += part

    @pl.when(step == 0)
    def _():
        add(mine_ref)

    @pl.when(step == 1)
    def _():
        add(other_ref)


def hop_apply(pos, counts, near, mine, other, pieces):
    chips, hops, rows, width = mine.shape
    bands = pieces.shape[2]
    picks = [
        pl.BlockSpec(
            (1, width, bands), lambda s, k, pos, cnt, near, i=i: (near[pos[1], i], 0, 0)
        )
        for i in range(hops)
    ]
    block = (chips, 1, rows, width)
    return pl.pallas_call(
        hop_kernel,
        out_shape=jax.ShapeDtypeStruct((chips, CORES, rows, bands), jnp.float32),
        grid_spec=pltpu.PrefetchScalarGridSpec(
            num_scalar_prefetch=3,
            grid=(CORES, hops),
            in_specs=[
                pl.BlockSpec(block, lambda s, k, *_: (0, jnp.where(s == 0, k, hops - 1), 0, 0)),
                pl.BlockSpec(block, lambda s, k, *_: (0, jnp.where(s == 0, 0, k), 0, 0)),
            ]
            + picks,
            out_specs=pl.BlockSpec(
                (chips, 1, rows, bands), lambda s, k, pos, *_: (0, (pos[0] + s) % CORES, 0, 0)
            ),
            scratch_shapes=[pltpu.VMEM((hops, width, bands), jnp.bfloat16)],
        ),
        compiler_params=pltpu.CompilerParams(vmem_limit_bytes=40 << 20),
        cost_estimate=pl.CostEstimate(
            flops=4 * mine.size * bands,
            bytes_accessed=4 * mine.size + 2 * hops * width * bands,
            transcendentals=0,
        ),
        name="hop_apply",
    )(pos, counts, near, mine, other, *([pieces] * hops))


def own_kernel(pos, counts, mine_ref, other_ref, x_ref, h_ref, o_ref, masked):
    step = pl.program_id(0)
    chips, _, rows, bands = o_ref.shape
    width = masked.shape[0]
    count = counts[pos[1]]

    @pl.when(step == 0)
    def _():
        masked_copy(masked, x_ref[0], count)

    def finish(a_ref):
        lhs = a_ref[...].reshape(-1, width)
        part = jnp.dot(lhs, masked[...], preferred_element_type=jnp.float32)
        total = part.reshape(o_ref.shape) + h_ref[...]
        core = (pos[0] + step) % CORES
        at = lax.broadcasted_iota(jnp.int32, o_ref.shape, 0) * (CORES * rows)
        at = at + core * rows + lax.broadcasted_iota(jnp.int32, o_ref.shape, 2)
        o_ref[...] = jnp.where(at < count, total, jnp.zeros_like(total))

    @pl.when(step == 0)
    def _():
        finish(mine_ref)

    @pl.when(step == 1)
    def _():
        finish(other_ref)


def own_apply(pos, counts, mine, other, coeffs, hopped):
    chips, rows, width = mine.shape
    bands = coeffs.shape[2]

    def out_map(s, pos, counts):
        return (0, (pos[0] + s) % CORES, 0, 0)

    whole = pl.BlockSpec((chips, rows, width), lambda s, *_: (0, 0, 0))
    return pl.pallas_call(
        own_kernel,
        out_shape=jax.ShapeDtypeStruct(hopped.shape, jnp.float32),
        grid_spec=pltpu.PrefetchScalarGridSpec(
            num_scalar_prefetch=2,
            grid=(CORES,),
            in_specs=[
                whole,
                whole,
                pl.BlockSpec((1, width, bands), lambda s, *_: (0, 0, 0)),
                pl.BlockSpec((chips, 1, rows, bands), out_map),
            ],
            out_specs=pl.BlockSpec((chips, 1, rows, bands), out_map),
            scratch_shapes=[pltpu.VMEM((width, bands), jnp.bfloat16)],
        ),
        compiler_params=pltpu.CompilerParams(vmem_limit_bytes=40 << 20),
        cost_estimate=pl.CostEstimate(
            flops=4 * mine.size * bands,
            bytes_accessed=4 * mine.size + 2 * width * bands + 8 * hopped.size,
            transcendentals=0,
        ),
        name="own_apply",
    )(pos, counts, mine, other, coeffs, hopped)


def local(basis_values, basis_derivs, potential, hop_blocks, coeffs, counts, neighbours):
    pos = jnp.stack([lax.axis_index("c"), lax.axis_index(ELEM)]).astype(jnp.int32)
    basis_values, pos = lax.optimization_barrier((basis_values, pos))
    values = slab(basis_values[0])
    derivs = slab(basis_derivs[0])

    pieces = lax.all_gather(coeffs, "zh", axis=0, tiled=True)
    pieces = lax.all_gather(pieces, "y", axis=0, tiled=True)
    hops = lax.all_gather(hop_blocks[0], CHIPS, axis=0, tiled=False)
    hopped = hop_apply(pos, counts, neighbours, hops, swap_cores(hops), pieces)

    weighted = (potential[0][None, :] * values.astype(jnp.float32)).astype(jnp.bfloat16)
    part = jnp.einsum("ip,jp->ij", values, weighted, preferred_element_type=jnp.float32)
    part = part + 0.5 * jnp.einsum(
        "ip,jp->ij", derivs, derivs, preferred_element_type=jnp.float32
    )

    chips = lax.axis_size(CHIPS)
    width = part.shape[0]
    rows = width // (chips * CORES)
    part = part.reshape(chips, CORES, rows, width).transpose(1, 0, 2, 3)
    part = lax.all_to_all(part, "c", 0, 0, tiled=True).sum(0)
    part = lax.all_to_all(part, CHIPS, 0, 0, tiled=True).sum(0)
    low = spread(part.astype(jnp.bfloat16))
    result = own_apply(pos, counts, low, swap_cores(low), coeffs, hopped)
    return result.reshape(1, width, coeffs.shape[2])


def solution(mesh):
    fine = Mesh(mesh.devices.reshape(4, 4, 2, 4, 2), ("y", "zh", "zl", "x", "c"))
    placed = (
        P(ELEM, GRP, None),
        P(ELEM, GRP, None),
        P(ELEM, GRP),
        P(ELEM, None, GRP, None),
        P(ELEM, None, GRP),
        P(),
        P(),
    )
    return jax.shard_map(
        local, mesh=fine, in_specs=placed, out_specs=P(ELEM, None, GRP), check_vma=False
    )
```

```python
import jax
import jax.numpy as jnp
from jax import lax
from jax.experimental import pallas as pl
from jax.experimental.pallas import tpu as pltpu
from jax.sharding import Mesh, PartitionSpec as P

ELEM = ("y", "zh")
CHIPS = ("zl", "x")
GRP = ("zl", "x", "c")
CORES = 2
SIDE = 4


def swap_cores(a):
    return lax.ppermute(a, "c", [(0, 1), (1, 0)])


def shift(a, axis, step):
    size = lax.axis_size(axis)
    return lax.ppermute(a, axis, [((i + step) % size, i) for i in range(size)])


def far(after, before, axis):
    size = lax.axis_size(axis)
    held = jnp.where(lax.axis_index("c") == 0, after, before)
    pairs = []
    for i in range(size):
        pairs.append((((i + 1) % size) * CORES, i * CORES))
        pairs.append((((i - 1) % size) * CORES + 1, i * CORES + 1))
    return lax.ppermute(held, (axis, "c"), pairs)


def split_kernel(a_ref, o_ref, sems):
    devices, _, points = o_ref.shape
    copies = [
        pltpu.make_async_copy(a_ref.at[:, pl.ds(i * points, points)], o_ref.at[i], sems.at[i])
        for i in range(devices)
    ]
    for copy in copies:
        copy.start()
    for copy in copies:
        copy.wait()


def split_points(a):
    rows, points = a.shape
    devices = lax.axis_size(GRP)
    return pl.pallas_call(
        split_kernel,
        out_shape=jax.ShapeDtypeStruct((devices, rows, points // devices), a.dtype),
        in_specs=[pl.BlockSpec(memory_space=pltpu.HBM)],
        out_specs=pl.BlockSpec(memory_space=pltpu.VMEM),
        scratch_shapes=[pltpu.SemaphoreType.DMA((devices,))],
        cost_estimate=pl.CostEstimate(flops=0, bytes_accessed=4 * a.size, transcendentals=0),
        name="split_points",
    )(a)


def triangle(side):
    return [j * (j + 1) // 2 for j in range(side)]


def value_kernel(p_ref, v_ref, o_ref):
    size = o_ref.shape[1]
    for j, first in enumerate(triangle(SIDE)):
        v = v_ref[pl.ds(j * size, size), :].astype(jnp.float32)
        w = (p_ref[...] * v).astype(jnp.bfloat16)
        d = lax.dot_general(
            v_ref[pl.ds(0, (j + 1) * size), :],
            w,
            (((1,), (1,)), ((), ())),
            preferred_element_type=jnp.float32,
        )
        o_ref[pl.ds(first, j + 1)] = d.reshape(j + 1, size, size)


def value_part(potential, values):
    rows, points = values.shape
    size = rows // SIDE
    blocks = SIDE * (SIDE + 1) // 2
    return pl.pallas_call(
        value_kernel,
        out_shape=jax.ShapeDtypeStruct((blocks, size, size), jnp.float32),
        compiler_params=pltpu.CompilerParams(vmem_limit_bytes=40 << 20),
        cost_estimate=pl.CostEstimate(
            flops=2 * blocks * size * size * points,
            bytes_accessed=2 * values.size + 4 * blocks * size * size,
            transcendentals=0,
        ),
        name="value_part",
    )(potential, values)


def deriv_kernel(pos, d_ref, g_ref, keep_ref, send_ref):
    size = g_ref.shape[1]
    half = size // CORES
    first_core = pos[0] == 0
    for j, first in enumerate(triangle(SIDE)):
        d = lax.dot_general(
            d_ref[pl.ds(0, (j + 1) * size), :],
            d_ref[pl.ds(j * size, size), :],
            (((1,), (1,)), ((), ())),
            preferred_element_type=jnp.float32,
        )
        d = 0.5 * d.reshape(j + 1, size, size) + g_ref[pl.ds(first, j + 1)]
        top, bottom = d[:, :half], d[:, half:]
        for ref, part in (
            (keep_ref, jnp.where(first_core, top, bottom)),
            (send_ref, jnp.where(first_core, bottom, top)),
        ):
            chips, _, rows, _ = ref.shape
            part = part.reshape(j + 1, chips, rows, size)
            for i in range(j + 1):
                ref[:, first + i] = part[i]


def deriv_part(pos, derivs, partial):
    blocks, size, _ = partial.shape
    chips = lax.axis_size(CHIPS)
    out = jax.ShapeDtypeStruct((chips, blocks, size // CORES // chips, size), jnp.float32)
    vmem = pl.BlockSpec(memory_space=pltpu.VMEM)
    return pl.pallas_call(
        deriv_kernel,
        out_shape=(out, out),
        in_specs=[pl.BlockSpec(memory_space=pltpu.SMEM), vmem, vmem],
        compiler_params=pltpu.CompilerParams(vmem_limit_bytes=40 << 20),
        cost_estimate=pl.CostEstimate(
            flops=2 * partial.size * derivs.shape[1],
            bytes_accessed=2 * derivs.size + 8 * partial.size,
            transcendentals=0,
        ),
        name="deriv_part",
    )(pos, derivs, partial)


def masked_copy(src, count):
    rows = lax.broadcasted_iota(jnp.int32, src.shape, 0)
    src = src.astype(jnp.float32)
    return jnp.where(rows < count, src, jnp.zeros_like(src)).astype(jnp.bfloat16)


def hop_places(pos):
    places = []
    for core in (pos[0], 1 - pos[0]):
        for dx in (0, 1, 3, 2):
            for zl in (pos[4], 1 - pos[4]):
                places.append((zl * 4 + ((pos[5] + dx) & 3)) * CORES + core)
    return places


def hop_kernel(pos, counts, near, *refs):
    hop_refs, piece_refs = refs[:16], refs[16:-5]
    o_ref, hops, near_coeffs, hop_sem, near_sem = refs[-5:]
    many, _, rows, width = hops.shape
    places = hop_places(pos)
    copies = [
        pltpu.make_async_copy(ref.at[0], hops.at[:, places[i]], hop_sem.at[i])
        for i, ref in enumerate(hop_refs)
    ]
    for copy in copies:
        copy.start()
    stacked, opposite = piece_refs[:4], piece_refs[4:]
    for k in range(many):
        element = near[pos[1], k]
        dy = ((element >> 2) - pos[2]) & 3
        dz = ((element & 3) - pos[3]) & 3
        for z in range(4):
            for y in range(4):
                piece = opposite[y].at[0] if z == 2 else stacked[y].at[(0, 1, 0, 2)[z]]

                @pl.when((dz == z) & (dy == y))
                def _():
                    pltpu.make_async_copy(piece, near_coeffs.at[k], near_sem.at[k]).start()

    for copy in copies:
        copy.wait()
    for k in range(many):
        pltpu.make_async_copy(piece_refs[0].at[0], near_coeffs.at[k], near_sem.at[k]).wait()
        x = masked_copy(near_coeffs[k], counts[near[pos[1], k]])
        part = jnp.dot(hops[k].reshape(-1, width), x, preferred_element_type=jnp.float32)
        if k == 0:
            o_ref[...] = part
        else:
            o_ref[...] += part


def hop_apply(pos, counts, near, hops, pieces):
    _, many, rows, width = hops[0].shape
    blocks = len(hops)
    bands = pieces[0].shape[2]
    smem = pl.BlockSpec(memory_space=pltpu.SMEM)
    return pl.pallas_call(
        hop_kernel,
        out_shape=jax.ShapeDtypeStruct((blocks * rows, bands), jnp.float32),
        in_specs=[smem] * 3 + [pl.BlockSpec(memory_space=pltpu.HBM)] * (len(hops) + len(pieces)),
        scratch_shapes=[
            pltpu.VMEM((many, blocks, rows, width), jnp.bfloat16),
            pltpu.VMEM((many, width, bands), jnp.bfloat16),
            pltpu.SemaphoreType.DMA((blocks,)),
            pltpu.SemaphoreType.DMA((many,)),
        ],
        compiler_params=pltpu.CompilerParams(vmem_limit_bytes=60 << 20),
        cost_estimate=pl.CostEstimate(
            flops=2 * len(hops) * hops[0].size * bands,
            bytes_accessed=2 * len(hops) * hops[0].size + 2 * many * width * bands,
            transcendentals=0,
        ),
        name="hop_apply",
    )(pos, counts, near, *hops, *pieces)


def own_kernel(pos, counts, mine_ref, other_ref, x_ref, h_ref, o_ref, low):
    chips, blocks, rows, size = mine_ref.shape
    half = size // CORES
    for ref, core in ((mine_ref, pos[0]), (other_ref, 1 - pos[0])):
        at = pl.multiple_of(core * half, half)
        for g in range(chips):
            low[:, pl.ds(at + g * rows, rows), :] = ref[g]
    count = counts[pos[1]]
    x = masked_copy(x_ref[0], count)
    o_ref[...] = h_ref[...]
    for j, first in enumerate(triangle(SIDE)):
        column = low[pl.ds(first, j + 1)].reshape((j + 1) * size, size)
        here = pl.ds(j * size, size)
        o_ref[pl.ds(0, (j + 1) * size), :] += jnp.dot(
            column, x[j * size : (j + 1) * size], preferred_element_type=jnp.float32
        )
        if j:
            o_ref[here, :] += lax.dot_general(
                column[: j * size],
                x[: j * size],
                (((0,), (0,)), ((), ())),
                preferred_element_type=jnp.float32,
            )
    at = lax.broadcasted_iota(jnp.int32, o_ref.shape, 0)
    o_ref[...] = jnp.where(at < count, o_ref[...], jnp.zeros_like(o_ref))


def own_apply(pos, counts, mine, other, coeffs, hopped):
    chips, blocks, rows, size = mine.shape
    smem, vmem = pl.BlockSpec(memory_space=pltpu.SMEM), pl.BlockSpec(memory_space=pltpu.VMEM)
    return pl.pallas_call(
        own_kernel,
        out_shape=jax.ShapeDtypeStruct(hopped.shape, jnp.float32),
        in_specs=[smem, smem] + [vmem] * 4,
        scratch_shapes=[pltpu.VMEM((blocks, size, size), jnp.bfloat16)],
        compiler_params=pltpu.CompilerParams(vmem_limit_bytes=40 << 20),
        cost_estimate=pl.CostEstimate(
            flops=2 * coeffs.shape[1] ** 2 * coeffs.shape[2],
            bytes_accessed=4 * mine.size + 2 * coeffs.size + 8 * hopped.size,
            transcendentals=0,
        ),
        name="own_apply",
    )(pos, counts, mine, other, coeffs, hopped)


def local(basis_values, basis_derivs, potential, hop_blocks, coeffs, counts, neighbours):
    pos = [lax.axis_index(n) for n in ("c", ELEM, "y", "zh", "zl", "x")]
    pos = jnp.stack(pos).astype(jnp.int32)
    basis_values, pos = lax.optimization_barrier((basis_values, pos))

    def exchange(a):
        return lax.all_to_all(a, GRP, 0, 0, tiled=True)

    barrier = lax.optimization_barrier
    pair = shift(hop_blocks, "zl", 1)
    own_x = [shift(hop_blocks, "x", 1), shift(hop_blocks, "x", 3)]
    pair, own_x, ring = barrier((pair, own_x, coeffs))
    after, before = shift(ring, "zh", 1), shift(ring, "zh", 3)
    pair_x = [shift(pair, "x", 1), shift(pair, "x", 3)]
    own_far = far(*own_x, "x")
    values, after, before, pair_x, own_far = barrier(
        (split_points(basis_values[0]), after, before, pair_x, own_far)
    )

    values = exchange(values)
    stacked = jnp.concatenate([coeffs, after, before])
    opposite = far(after, before, "zh")
    near_y = [shift(stacked, "y", 1), shift(stacked, "y", 3)]
    pair_far = far(*pair_x, "x")
    derivs, opposite, near_y, pair_far = barrier(
        (split_points(basis_derivs[0]), opposite, near_y, pair_far)
    )

    derivs = exchange(derivs)
    far_y = far(*near_y, "y")
    near_o = [shift(opposite, "y", 1), shift(opposite, "y", 3)]
    pieces = [stacked, near_y[0], far_y, near_y[1]]
    pieces += [opposite, near_o[0], far(*near_o, "y"), near_o[1]]
    hops = [hop_blocks, pair, own_x[0], pair_x[0], own_x[1], pair_x[1], own_far, pair_far]
    others = [swap_cores(h) for h in hops]
    hopped = hop_apply(pos, counts, neighbours, hops + others, pieces)
    width = coeffs.shape[1]
    part = value_part(potential, values.reshape(width, -1))
    derivs, hopped, part = barrier((derivs, hopped, part))

    keep, send = deriv_part(pos, derivs.reshape(width, -1), part)
    part = keep + swap_cores(send)
    part = lax.all_to_all(part, CHIPS, 0, 0, tiled=True).sum(0).astype(jnp.bfloat16)
    chips = lax.axis_size(CHIPS)
    low = jnp.broadcast_to(part[None], (chips, *part.shape))
    low = lax.all_to_all(low, CHIPS, 0, 0, tiled=True)
    result = own_apply(pos, counts, low, swap_cores(low), coeffs, hopped)
    return result[None]


def solution(mesh):
    fine = Mesh(mesh.devices.reshape(4, 4, 2, 4, 2), ("y", "zh", "zl", "x", "c"))
    placed = (
        P(ELEM, GRP, None),
        P(ELEM, GRP, None),
        P(ELEM, GRP),
        P(ELEM, None, GRP, None),
        P(ELEM, None, GRP),
        P(),
        P(),
    )
    return jax.shard_map(
        local, mesh=fine, in_specs=placed, out_specs=P(ELEM, None, GRP), check_vma=False
    )
```

```python
import jax
import jax.numpy as jnp
from jax import lax
from jax.experimental import pallas as pl
from jax.experimental.pallas import tpu as pltpu
from jax.sharding import Mesh, PartitionSpec as P

ELEM = ("y", "zh")
CHIPS = ("zl", "x")
GRP = ("zl", "x", "c")
CORES = 2
SIDE = 4


def swap_cores(a):
    return lax.ppermute(a, "c", [(0, 1), (1, 0)])


def shift(a, axis, step):
    size = lax.axis_size(axis)
    return lax.ppermute(a, axis, [((i + step) % size, i) for i in range(size)])


def far(after, before, axis):
    size = lax.axis_size(axis)
    held = jnp.where(lax.axis_index("c") == 0, after, before)
    pairs = []
    for i in range(size):
        pairs.append((((i + 1) % size) * CORES, i * CORES))
        pairs.append((((i - 1) % size) * CORES + 1, i * CORES + 1))
    return lax.ppermute(held, (axis, "c"), pairs)


def split_kernel(a_ref, o_ref, sems):
    devices, _, points = o_ref.shape
    copies = [
        pltpu.make_async_copy(a_ref.at[:, pl.ds(i * points, points)], o_ref.at[i], sems.at[i])
        for i in range(devices)
    ]
    for copy in copies:
        copy.start()
    for copy in copies:
        copy.wait()


def split_points(a):
    rows, points = a.shape
    devices = lax.axis_size(GRP)
    return pl.pallas_call(
        split_kernel,
        out_shape=jax.ShapeDtypeStruct((devices, rows, points // devices), a.dtype),
        in_specs=[pl.BlockSpec(memory_space=pltpu.HBM)],
        out_specs=pl.BlockSpec(memory_space=pltpu.VMEM),
        scratch_shapes=[pltpu.SemaphoreType.DMA((devices,))],
        cost_estimate=pl.CostEstimate(flops=0, bytes_accessed=4 * a.size, transcendentals=0),
        name="split_points",
    )(a)


def triangle(side):
    return [j * (j + 1) // 2 for j in range(side)]


def value_kernel(p_ref, v_ref, o_ref):
    size = o_ref.shape[1]
    for j, first in enumerate(triangle(SIDE)):
        v = v_ref[pl.ds(j * size, size), :].astype(jnp.float32)
        w = (p_ref[...] * v).astype(jnp.bfloat16)
        d = lax.dot_general(
            v_ref[pl.ds(0, (j + 1) * size), :],
            w,
            (((1,), (1,)), ((), ())),
            preferred_element_type=jnp.float32,
        )
        o_ref[pl.ds(first, j + 1)] = d.reshape(j + 1, size, size)


def value_part(potential, values):
    rows, points = values.shape
    size = rows // SIDE
    blocks = SIDE * (SIDE + 1) // 2
    return pl.pallas_call(
        value_kernel,
        out_shape=jax.ShapeDtypeStruct((blocks, size, size), jnp.float32),
        compiler_params=pltpu.CompilerParams(vmem_limit_bytes=40 << 20),
        cost_estimate=pl.CostEstimate(
            flops=2 * blocks * size * size * points,
            bytes_accessed=2 * values.size + 4 * blocks * size * size,
            transcendentals=0,
        ),
        name="value_part",
    )(potential, values)


def deriv_kernel(pos, d_ref, g_ref, keep_ref, send_ref):
    size = g_ref.shape[1]
    half = size // CORES
    first_core = pos[0] == 0
    for j, first in enumerate(triangle(SIDE)):
        d = lax.dot_general(
            d_ref[pl.ds(0, (j + 1) * size), :],
            d_ref[pl.ds(j * size, size), :],
            (((1,), (1,)), ((), ())),
            preferred_element_type=jnp.float32,
        )
        d = 0.5 * d.reshape(j + 1, size, size) + g_ref[pl.ds(first, j + 1)]
        top, bottom = d[:, :half], d[:, half:]
        for ref, part in (
            (keep_ref, jnp.where(first_core, top, bottom)),
            (send_ref, jnp.where(first_core, bottom, top)),
        ):
            chips, _, rows, _ = ref.shape
            part = part.reshape(j + 1, chips, rows, size)
            for i in range(j + 1):
                ref[:, first + i] = part[i]


def deriv_part(pos, derivs, partial):
    blocks, size, _ = partial.shape
    chips = lax.axis_size(CHIPS)
    out = jax.ShapeDtypeStruct((chips, blocks, size // CORES // chips, size), jnp.float32)
    vmem = pl.BlockSpec(memory_space=pltpu.VMEM)
    return pl.pallas_call(
        deriv_kernel,
        out_shape=(out, out),
        in_specs=[pl.BlockSpec(memory_space=pltpu.SMEM), vmem, vmem],
        compiler_params=pltpu.CompilerParams(vmem_limit_bytes=40 << 20),
        cost_estimate=pl.CostEstimate(
            flops=2 * partial.size * derivs.shape[1],
            bytes_accessed=2 * derivs.size + 8 * partial.size,
            transcendentals=0,
        ),
        name="deriv_part",
    )(pos, derivs, partial)


def masked_copy(src, count):
    rows = lax.broadcasted_iota(jnp.int32, src.shape, 0)
    src = src.astype(jnp.float32)
    return jnp.where(rows < count, src, jnp.zeros_like(src)).astype(jnp.bfloat16)


def hop_places(pos):
    places = []
    for core in (pos[0], 1 - pos[0]):
        for dx in (0, 1, 3, 2):
            for zl in (pos[4], 1 - pos[4]):
                places.append((zl * 4 + ((pos[5] + dx) & 3)) * CORES + core)
    return places


def hop_kernel(pos, counts, near, *refs):
    hop_refs, piece_refs = refs[:16], refs[16:-5]
    o_ref, hops, near_coeffs, hop_sem, near_sem = refs[-5:]
    many, _, rows, width = hops.shape
    places = hop_places(pos)
    copies = [
        pltpu.make_async_copy(ref.at[0], hops.at[:, places[i]], hop_sem.at[i])
        for i, ref in enumerate(hop_refs)
    ]
    for copy in copies:
        copy.start()
    stacked, opposite = piece_refs[:4], piece_refs[4:]
    for k in range(many):
        element = near[pos[1], k]
        dy = ((element >> 2) - pos[2]) & 3
        dz = ((element & 3) - pos[3]) & 3
        for z in range(4):
            for y in range(4):
                piece = opposite[y].at[0] if z == 2 else stacked[y].at[(0, 1, 0, 2)[z]]

                @pl.when((dz == z) & (dy == y))
                def _():
                    pltpu.make_async_copy(piece, near_coeffs.at[k], near_sem.at[k]).start()

    for copy in copies:
        copy.wait()
    for k in range(many):
        pltpu.make_async_copy(piece_refs[0].at[0], near_coeffs.at[k], near_sem.at[k]).wait()
        x = masked_copy(near_coeffs[k], counts[near[pos[1], k]])
        part = jnp.dot(hops[k].reshape(-1, width), x, preferred_element_type=jnp.float32)
        if k == 0:
            o_ref[...] = part
        else:
            o_ref[...] += part


def hop_apply(pos, counts, near, hops, pieces):
    _, many, rows, width = hops[0].shape
    blocks = len(hops)
    bands = pieces[0].shape[2]
    smem = pl.BlockSpec(memory_space=pltpu.SMEM)
    return pl.pallas_call(
        hop_kernel,
        out_shape=jax.ShapeDtypeStruct((blocks * rows, bands), jnp.float32),
        in_specs=[smem] * 3 + [pl.BlockSpec(memory_space=pltpu.HBM)] * (len(hops) + len(pieces)),
        scratch_shapes=[
            pltpu.VMEM((many, blocks, rows, width), jnp.bfloat16),
            pltpu.VMEM((many, width, bands), jnp.bfloat16),
            pltpu.SemaphoreType.DMA((blocks,)),
            pltpu.SemaphoreType.DMA((many,)),
        ],
        compiler_params=pltpu.CompilerParams(vmem_limit_bytes=60 << 20),
        cost_estimate=pl.CostEstimate(
            flops=2 * len(hops) * hops[0].size * bands,
            bytes_accessed=2 * len(hops) * hops[0].size + 2 * many * width * bands,
            transcendentals=0,
        ),
        name="hop_apply",
    )(pos, counts, near, *hops, *pieces)


def own_kernel(pos, counts, mine_ref, other_ref, x_ref, h_ref, o_ref, low):
    chips, blocks, rows, size = mine_ref.shape
    half = size // CORES
    for ref, core in ((mine_ref, pos[0]), (other_ref, 1 - pos[0])):
        at = pl.multiple_of(core * half, half)
        for g in range(chips):
            low[:, pl.ds(at + g * rows, rows), :] = ref[g]
    count = counts[pos[1]]
    x = masked_copy(x_ref[0], count)
    o_ref[...] = h_ref[...]
    for j, first in enumerate(triangle(SIDE)):
        column = low[pl.ds(first, j + 1)].reshape((j + 1) * size, size)
        here = pl.ds(j * size, size)
        o_ref[pl.ds(0, (j + 1) * size), :] += jnp.dot(
            column, x[j * size : (j + 1) * size], preferred_element_type=jnp.float32
        )
        if j:
            o_ref[here, :] += lax.dot_general(
                column[: j * size],
                x[: j * size],
                (((0,), (0,)), ((), ())),
                preferred_element_type=jnp.float32,
            )
    at = lax.broadcasted_iota(jnp.int32, o_ref.shape, 0)
    o_ref[...] = jnp.where(at < count, o_ref[...], jnp.zeros_like(o_ref))


def own_apply(pos, counts, mine, other, coeffs, hopped):
    chips, blocks, rows, size = mine.shape
    smem, vmem = pl.BlockSpec(memory_space=pltpu.SMEM), pl.BlockSpec(memory_space=pltpu.VMEM)
    return pl.pallas_call(
        own_kernel,
        out_shape=jax.ShapeDtypeStruct(hopped.shape, jnp.float32),
        in_specs=[smem, smem] + [vmem] * 4,
        scratch_shapes=[pltpu.VMEM((blocks, size, size), jnp.bfloat16)],
        compiler_params=pltpu.CompilerParams(vmem_limit_bytes=40 << 20),
        cost_estimate=pl.CostEstimate(
            flops=2 * coeffs.shape[1] ** 2 * coeffs.shape[2],
            bytes_accessed=4 * mine.size + 2 * coeffs.size + 8 * hopped.size,
            transcendentals=0,
        ),
        name="own_apply",
    )(pos, counts, mine, other, coeffs, hopped)


def local(basis_values, basis_derivs, potential, hop_blocks, coeffs, counts, neighbours):
    pos = [lax.axis_index(n) for n in ("c", ELEM, "y", "zh", "zl", "x")]
    pos = jnp.stack(pos).astype(jnp.int32)
    basis_values, pos = lax.optimization_barrier((basis_values, pos))

    def exchange(a):
        return lax.all_to_all(a, GRP, 0, 0, tiled=True)

    barrier = lax.optimization_barrier
    pair = shift(hop_blocks, "zl", 1)
    own_x = [shift(hop_blocks, "x", 1), shift(hop_blocks, "x", 3)]
    pair, own_x, ring = barrier((pair, own_x, coeffs))
    after, before = shift(ring, "zh", 1), shift(ring, "zh", 3)
    pair_x = [shift(pair, "x", 1), shift(pair, "x", 3)]
    own_far = far(*own_x, "x")
    values, after, before, pair_x, own_far = barrier(
        (split_points(basis_values[0]), after, before, pair_x, own_far)
    )

    values = exchange(values)
    stacked = jnp.concatenate([coeffs, after, before])
    opposite = far(after, before, "zh")
    near_y = [shift(stacked, "y", 1), shift(stacked, "y", 3)]
    pair_far = far(*pair_x, "x")
    derivs, opposite, near_y, pair_far = barrier(
        (split_points(basis_derivs[0]), opposite, near_y, pair_far)
    )

    derivs = exchange(derivs)
    far_y = far(*near_y, "y")
    near_o = [shift(opposite, "y", 1), shift(opposite, "y", 3)]
    pieces = [stacked, near_y[0], far_y, near_y[1]]
    pieces += [opposite, near_o[0], far(*near_o, "y"), near_o[1]]
    hops = [hop_blocks, pair, own_x[0], pair_x[0], own_x[1], pair_x[1], own_far, pair_far]
    others = [swap_cores(h) for h in hops]
    hopped = hop_apply(pos, counts, neighbours, hops + others, pieces)
    width = coeffs.shape[1]
    part = value_part(potential, values.reshape(width, -1))
    derivs, hopped, part = barrier((derivs, hopped, part))

    keep, send = deriv_part(pos, derivs.reshape(width, -1), part)
    part = (keep + swap_cores(send)).astype(jnp.bfloat16)
    part = lax.all_to_all(part, CHIPS, 0, 0, tiled=True).astype(jnp.float32)
    part = part.sum(0).astype(jnp.bfloat16)
    chips = lax.axis_size(CHIPS)
    low = jnp.broadcast_to(part[None], (chips, *part.shape))
    low = lax.all_to_all(low, CHIPS, 0, 0, tiled=True)
    result = own_apply(pos, counts, low, swap_cores(low), coeffs, hopped)
    return result[None]


def solution(mesh):
    fine = Mesh(mesh.devices.reshape(4, 4, 2, 4, 2), ("y", "zh", "zl", "x", "c"))
    placed = (
        P(ELEM, GRP, None),
        P(ELEM, GRP, None),
        P(ELEM, GRP),
        P(ELEM, None, GRP, None),
        P(ELEM, None, GRP),
        P(),
        P(),
    )
    return jax.shard_map(
        local, mesh=fine, in_specs=placed, out_specs=P(ELEM, None, GRP), check_vma=False
    )
```

```python
import jax
import jax.numpy as jnp
from jax import lax
from jax.experimental import pallas as pl
from jax.experimental.pallas import tpu as pltpu
from jax.sharding import Mesh, PartitionSpec as P

ELEM = ("y", "zh")
CHIPS = ("zl", "x")
GRP = ("zl", "x", "c")
CORES = 2
SIDE = 4


def swap_cores(a):
    return lax.ppermute(a, "c", [(0, 1), (1, 0)])


def shift(a, axis, step):
    size = lax.axis_size(axis)
    return lax.ppermute(a, axis, [((i + step) % size, i) for i in range(size)])


def far(after, before, axis):
    size = lax.axis_size(axis)
    held = jnp.where(lax.axis_index("c") == 0, after, before)
    pairs = []
    for i in range(size):
        pairs.append((((i + 1) % size) * CORES, i * CORES))
        pairs.append((((i - 1) % size) * CORES + 1, i * CORES + 1))
    return lax.ppermute(held, (axis, "c"), pairs)


def split_kernel(a_ref, o_ref, sems):
    devices, _, points = o_ref.shape
    copies = [
        pltpu.make_async_copy(a_ref.at[:, pl.ds(i * points, points)], o_ref.at[i], sems.at[i])
        for i in range(devices)
    ]
    for copy in copies:
        copy.start()
    for copy in copies:
        copy.wait()


def split_points(a):
    rows, points = a.shape
    devices = lax.axis_size(GRP)
    return pl.pallas_call(
        split_kernel,
        out_shape=jax.ShapeDtypeStruct((devices, rows, points // devices), a.dtype),
        in_specs=[pl.BlockSpec(memory_space=pltpu.HBM)],
        out_specs=pl.BlockSpec(memory_space=pltpu.VMEM),
        scratch_shapes=[pltpu.SemaphoreType.DMA((devices,))],
        cost_estimate=pl.CostEstimate(flops=0, bytes_accessed=4 * a.size, transcendentals=0),
        name="split_points",
    )(a)


def triangle(side):
    return [j * (j + 1) // 2 for j in range(side)]


def value_kernel(p_ref, v_ref, o_ref):
    size = o_ref.shape[1]
    for j, first in enumerate(triangle(SIDE)):
        v = v_ref[pl.ds(j * size, size), :].astype(jnp.float32)
        w = (p_ref[...] * v).astype(jnp.bfloat16)
        d = lax.dot_general(
            v_ref[pl.ds(0, (j + 1) * size), :],
            w,
            (((1,), (1,)), ((), ())),
            preferred_element_type=jnp.float32,
        )
        o_ref[pl.ds(first, j + 1)] = d.reshape(j + 1, size, size)


def value_part(potential, values):
    rows, points = values.shape
    size = rows // SIDE
    blocks = SIDE * (SIDE + 1) // 2
    return pl.pallas_call(
        value_kernel,
        out_shape=jax.ShapeDtypeStruct((blocks, size, size), jnp.float32),
        compiler_params=pltpu.CompilerParams(vmem_limit_bytes=40 << 20),
        cost_estimate=pl.CostEstimate(
            flops=2 * blocks * size * size * points,
            bytes_accessed=2 * values.size + 4 * blocks * size * size,
            transcendentals=0,
        ),
        name="value_part",
    )(potential, values)


def deriv_kernel(pos, d_ref, g_ref, keep_ref, send_ref):
    size = g_ref.shape[1]
    half = size // CORES
    first_core = pos[0] == 0
    for j, first in enumerate(triangle(SIDE)):
        d = lax.dot_general(
            d_ref[pl.ds(0, (j + 1) * size), :],
            d_ref[pl.ds(j * size, size), :],
            (((1,), (1,)), ((), ())),
            preferred_element_type=jnp.float32,
        )
        d = 0.5 * d.reshape(j + 1, size, size) + g_ref[pl.ds(first, j + 1)]
        top, bottom = d[:, :half], d[:, half:]
        for ref, part in (
            (keep_ref, jnp.where(first_core, top, bottom)),
            (send_ref, jnp.where(first_core, bottom, top)),
        ):
            chips, _, rows, _ = ref.shape
            part = part.reshape(j + 1, chips, rows, size)
            for i in range(j + 1):
                ref[:, first + i] = part[i]


def deriv_part(pos, derivs, partial):
    blocks, size, _ = partial.shape
    chips = lax.axis_size(CHIPS)
    out = jax.ShapeDtypeStruct((chips, blocks, size // CORES // chips, size), jnp.float32)
    vmem = pl.BlockSpec(memory_space=pltpu.VMEM)
    return pl.pallas_call(
        deriv_kernel,
        out_shape=(out, out),
        in_specs=[pl.BlockSpec(memory_space=pltpu.SMEM), vmem, vmem],
        compiler_params=pltpu.CompilerParams(vmem_limit_bytes=40 << 20),
        cost_estimate=pl.CostEstimate(
            flops=2 * partial.size * derivs.shape[1],
            bytes_accessed=2 * derivs.size + 8 * partial.size,
            transcendentals=0,
        ),
        name="deriv_part",
    )(pos, derivs, partial)


def masked_copy(src, count):
    rows = lax.broadcasted_iota(jnp.int32, src.shape, 0)
    src = src.astype(jnp.float32)
    return jnp.where(rows < count, src, jnp.zeros_like(src)).astype(jnp.bfloat16)


def hop_places(pos):
    places = []
    for core in (pos[0], 1 - pos[0]):
        for dx in (0, 1, 3, 2):
            for zl in (pos[4], 1 - pos[4]):
                places.append((zl * 4 + ((pos[5] + dx) & 3)) * CORES + core)
    return places


def hop_kernel(pos, counts, near, *refs):
    hop_refs, piece_refs = refs[:16], refs[16:-5]
    o_ref, hops, near_coeffs, hop_sem, near_sem = refs[-5:]
    many, _, rows, width = hops.shape
    places = hop_places(pos)
    copies = [
        pltpu.make_async_copy(ref.at[0], hops.at[:, places[i]], hop_sem.at[i])
        for i, ref in enumerate(hop_refs)
    ]
    for copy in copies:
        copy.start()
    stacked, opposite = piece_refs[:4], piece_refs[4:]
    for k in range(many):
        element = near[pos[1], k]
        dy = ((element >> 2) - pos[2]) & 3
        dz = ((element & 3) - pos[3]) & 3
        for z in range(4):
            for y in range(4):
                piece = opposite[y].at[0] if z == 2 else stacked[y].at[(0, 1, 0, 2)[z]]

                @pl.when((dz == z) & (dy == y))
                def _():
                    pltpu.make_async_copy(piece, near_coeffs.at[k], near_sem.at[k]).start()

    for copy in copies:
        copy.wait()
    for k in range(many):
        pltpu.make_async_copy(piece_refs[0].at[0], near_coeffs.at[k], near_sem.at[k]).wait()
        x = masked_copy(near_coeffs[k], counts[near[pos[1], k]])
        part = jnp.dot(hops[k].reshape(-1, width), x, preferred_element_type=jnp.float32)
        if k == 0:
            o_ref[...] = part
        else:
            o_ref[...] += part


def hop_apply(pos, counts, near, hops, pieces):
    _, many, rows, width = hops[0].shape
    blocks = len(hops)
    bands = pieces[0].shape[2]
    smem = pl.BlockSpec(memory_space=pltpu.SMEM)
    return pl.pallas_call(
        hop_kernel,
        out_shape=jax.ShapeDtypeStruct((blocks * rows, bands), jnp.float32),
        in_specs=[smem] * 3 + [pl.BlockSpec(memory_space=pltpu.HBM)] * (len(hops) + len(pieces)),
        scratch_shapes=[
            pltpu.VMEM((many, blocks, rows, width), jnp.bfloat16),
            pltpu.VMEM((many, width, bands), jnp.bfloat16),
            pltpu.SemaphoreType.DMA((blocks,)),
            pltpu.SemaphoreType.DMA((many,)),
        ],
        compiler_params=pltpu.CompilerParams(vmem_limit_bytes=60 << 20),
        cost_estimate=pl.CostEstimate(
            flops=2 * len(hops) * hops[0].size * bands,
            bytes_accessed=2 * len(hops) * hops[0].size + 2 * many * width * bands,
            transcendentals=0,
        ),
        name="hop_apply",
    )(pos, counts, near, *hops, *pieces)


def own_kernel(pos, counts, mine_ref, other_ref, x_ref, h_ref, o_ref, low):
    chips, blocks, rows, size = mine_ref.shape
    half = size // CORES
    for ref, core in ((mine_ref, pos[0]), (other_ref, 1 - pos[0])):
        at = pl.multiple_of(core * half, half)
        for g in range(chips):
            low[:, pl.ds(at + g * rows, rows), :] = ref[g]
    count = counts[pos[1]]
    x = masked_copy(x_ref[0], count)
    o_ref[...] = h_ref[...]
    for j, first in enumerate(triangle(SIDE)):
        column = low[pl.ds(first, j + 1)].reshape((j + 1) * size, size)
        here = pl.ds(j * size, size)
        o_ref[pl.ds(0, (j + 1) * size), :] += jnp.dot(
            column, x[j * size : (j + 1) * size], preferred_element_type=jnp.float32
        )
        if j:
            o_ref[here, :] += lax.dot_general(
                column[: j * size],
                x[: j * size],
                (((0,), (0,)), ((), ())),
                preferred_element_type=jnp.float32,
            )
    at = lax.broadcasted_iota(jnp.int32, o_ref.shape, 0)
    o_ref[...] = jnp.where(at < count, o_ref[...], jnp.zeros_like(o_ref))


def own_apply(pos, counts, mine, other, coeffs, hopped):
    chips, blocks, rows, size = mine.shape
    smem, vmem = pl.BlockSpec(memory_space=pltpu.SMEM), pl.BlockSpec(memory_space=pltpu.VMEM)
    return pl.pallas_call(
        own_kernel,
        out_shape=jax.ShapeDtypeStruct(hopped.shape, jnp.float32),
        in_specs=[smem, smem] + [vmem] * 4,
        scratch_shapes=[pltpu.VMEM((blocks, size, size), jnp.bfloat16)],
        compiler_params=pltpu.CompilerParams(vmem_limit_bytes=40 << 20),
        cost_estimate=pl.CostEstimate(
            flops=2 * coeffs.shape[1] ** 2 * coeffs.shape[2],
            bytes_accessed=4 * mine.size + 2 * coeffs.size + 8 * hopped.size,
            transcendentals=0,
        ),
        name="own_apply",
    )(pos, counts, mine, other, coeffs, hopped)


def local(basis_values, basis_derivs, potential, hop_blocks, coeffs, counts, neighbours):
    pos = [lax.axis_index(n) for n in ("c", ELEM, "y", "zh", "zl", "x")]
    pos = jnp.stack(pos).astype(jnp.int32)
    basis_values, pos = lax.optimization_barrier((basis_values, pos))

    def exchange(a):
        return lax.all_to_all(a, GRP, 0, 0, tiled=True)

    barrier = lax.optimization_barrier
    pair = shift(hop_blocks, "zl", 1)
    own_x = [shift(hop_blocks, "x", 1), shift(hop_blocks, "x", 3)]
    values, ring = barrier((split_points(basis_values[0]), coeffs))
    after, before = shift(ring, "zh", 1), shift(ring, "zh", 3)
    pair_x = [shift(pair, "x", 1), shift(pair, "x", 3)]
    own_far = far(*own_x, "x")
    values, after, before, pair_x, own_far = barrier(
        (values, after, before, pair_x, own_far)
    )

    values = exchange(values)
    stacked = jnp.concatenate([coeffs, after, before])
    opposite = far(after, before, "zh")
    near_y = [shift(stacked, "y", 1), shift(stacked, "y", 3)]
    pair_far = far(*pair_x, "x")
    derivs, opposite, near_y, pair_far = barrier(
        (split_points(basis_derivs[0]), opposite, near_y, pair_far)
    )

    derivs = exchange(derivs)
    far_y = far(*near_y, "y")
    near_o = [shift(opposite, "y", 1), shift(opposite, "y", 3)]
    pieces = [stacked, near_y[0], far_y, near_y[1]]
    pieces += [opposite, near_o[0], far(*near_o, "y"), near_o[1]]
    hops = [hop_blocks, pair, own_x[0], pair_x[0], own_x[1], pair_x[1], own_far, pair_far]
    others = [swap_cores(h) for h in hops]
    hopped = hop_apply(pos, counts, neighbours, hops + others, pieces)
    width = coeffs.shape[1]
    part = value_part(potential, values.reshape(width, -1))
    derivs, hopped, part = barrier((derivs, hopped, part))

    keep, send = deriv_part(pos, derivs.reshape(width, -1), part)
    part = (keep + swap_cores(send)).astype(jnp.bfloat16)
    part = lax.all_to_all(part, CHIPS, 0, 0, tiled=True).astype(jnp.float32)
    part = part.sum(0).astype(jnp.bfloat16)
    chips = lax.axis_size(CHIPS)
    low = jnp.broadcast_to(part[None], (chips, *part.shape))
    low = lax.all_to_all(low, CHIPS, 0, 0, tiled=True)
    result = own_apply(pos, counts, low, swap_cores(low), coeffs, hopped)
    return result[None]


def solution(mesh):
    fine = Mesh(mesh.devices.reshape(4, 4, 2, 4, 2), ("y", "zh", "zl", "x", "c"))
    placed = (
        P(ELEM, GRP, None),
        P(ELEM, GRP, None),
        P(ELEM, GRP),
        P(ELEM, None, GRP, None),
        P(ELEM, None, GRP),
        P(),
        P(),
    )
    return jax.shard_map(
        local, mesh=fine, in_specs=placed, out_specs=P(ELEM, None, GRP), check_vma=False
    )
```

```python
import jax
import jax.numpy as jnp
from jax import lax
from jax.experimental import pallas as pl
from jax.experimental.pallas import tpu as pltpu
from jax.sharding import Mesh, PartitionSpec as P

ELEM = ("y", "zh")
CHIPS = ("zl", "x")
GRP = ("zl", "x", "c")
CORES = 2
SIDE = 4


def swap_cores(a):
    return lax.ppermute(a, "c", [(0, 1), (1, 0)])


def shift(a, axis, step):
    size = lax.axis_size(axis)
    return lax.ppermute(a, axis, [((i + step) % size, i) for i in range(size)])


def far(after, before, axis):
    size = lax.axis_size(axis)
    held = jnp.where(lax.axis_index("c") == 0, after, before)
    pairs = []
    for i in range(size):
        pairs.append((((i + 1) % size) * CORES, i * CORES))
        pairs.append((((i - 1) % size) * CORES + 1, i * CORES + 1))
    return lax.ppermute(held, (axis, "c"), pairs)


def split_kernel(a_ref, o_ref, sems):
    devices, _, points = o_ref.shape
    copies = [
        pltpu.make_async_copy(a_ref.at[:, pl.ds(i * points, points)], o_ref.at[i], sems.at[i])
        for i in range(devices)
    ]
    for copy in copies:
        copy.start()
    for copy in copies:
        copy.wait()


def split_points(a):
    rows, points = a.shape
    devices = lax.axis_size(GRP)
    return pl.pallas_call(
        split_kernel,
        out_shape=jax.ShapeDtypeStruct((devices, rows, points // devices), a.dtype),
        in_specs=[pl.BlockSpec(memory_space=pltpu.HBM)],
        out_specs=pl.BlockSpec(memory_space=pltpu.VMEM),
        scratch_shapes=[pltpu.SemaphoreType.DMA((devices,))],
        cost_estimate=pl.CostEstimate(flops=0, bytes_accessed=4 * a.size, transcendentals=0),
        name="split_points",
    )(a)


def triangle(side):
    return [j * (j + 1) // 2 for j in range(side)]


def value_kernel(p_ref, v_ref, o_ref):
    size = o_ref.shape[1]
    for j, first in enumerate(triangle(SIDE)):
        v = v_ref[pl.ds(j * size, size), :].astype(jnp.float32)
        w = (p_ref[...] * v).astype(jnp.bfloat16)
        d = lax.dot_general(
            v_ref[pl.ds(0, (j + 1) * size), :],
            w,
            (((1,), (1,)), ((), ())),
            preferred_element_type=jnp.float32,
        )
        o_ref[pl.ds(first, j + 1)] = d.reshape(j + 1, size, size)


def value_part(potential, values):
    rows, points = values.shape
    size = rows // SIDE
    blocks = SIDE * (SIDE + 1) // 2
    return pl.pallas_call(
        value_kernel,
        out_shape=jax.ShapeDtypeStruct((blocks, size, size), jnp.float32),
        compiler_params=pltpu.CompilerParams(vmem_limit_bytes=40 << 20),
        cost_estimate=pl.CostEstimate(
            flops=2 * blocks * size * size * points,
            bytes_accessed=2 * values.size + 4 * blocks * size * size,
            transcendentals=0,
        ),
        name="value_part",
    )(potential, values)


def deriv_kernel(pos, d_ref, g_ref, keep_ref, send_ref):
    size = g_ref.shape[1]
    half = size // CORES
    first_core = pos[0] == 0
    for j, first in enumerate(triangle(SIDE)):
        d = lax.dot_general(
            d_ref[pl.ds(0, (j + 1) * size), :],
            d_ref[pl.ds(j * size, size), :],
            (((1,), (1,)), ((), ())),
            preferred_element_type=jnp.float32,
        )
        d = 0.5 * d.reshape(j + 1, size, size) + g_ref[pl.ds(first, j + 1)]
        top, bottom = d[:, :half], d[:, half:]
        for ref, part in (
            (keep_ref, jnp.where(first_core, top, bottom)),
            (send_ref, jnp.where(first_core, bottom, top)),
        ):
            chips, _, rows, _ = ref.shape
            part = part.reshape(j + 1, chips, rows, size)
            for i in range(j + 1):
                ref[:, first + i] = part[i]


def deriv_part(pos, derivs, partial):
    blocks, size, _ = partial.shape
    chips = lax.axis_size(CHIPS)
    out = jax.ShapeDtypeStruct((chips, blocks, size // CORES // chips, size), jnp.float32)
    vmem = pl.BlockSpec(memory_space=pltpu.VMEM)
    return pl.pallas_call(
        deriv_kernel,
        out_shape=(out, out),
        in_specs=[pl.BlockSpec(memory_space=pltpu.SMEM), vmem, vmem],
        compiler_params=pltpu.CompilerParams(vmem_limit_bytes=40 << 20),
        cost_estimate=pl.CostEstimate(
            flops=2 * partial.size * derivs.shape[1],
            bytes_accessed=2 * derivs.size + 8 * partial.size,
            transcendentals=0,
        ),
        name="deriv_part",
    )(pos, derivs, partial)


def masked_copy(src, count):
    rows = lax.broadcasted_iota(jnp.int32, src.shape, 0)
    src = src.astype(jnp.float32)
    return jnp.where(rows < count, src, jnp.zeros_like(src)).astype(jnp.bfloat16)


def hop_places(pos):
    places = []
    for core in (pos[0], 1 - pos[0]):
        for dx in (0, 1, 3, 2):
            for zl in (pos[4], 1 - pos[4]):
                places.append((zl * 4 + ((pos[5] + dx) & 3)) * CORES + core)
    return places


def hop_kernel(pos, counts, near, *refs):
    hop_refs, piece_refs = refs[:16], refs[16:-5]
    o_ref, hops, near_coeffs, hop_sem, near_sem = refs[-5:]
    many, _, rows, width = hops.shape
    places = hop_places(pos)
    copies = [
        pltpu.make_async_copy(ref.at[0], hops.at[:, places[i]], hop_sem.at[i])
        for i, ref in enumerate(hop_refs)
    ]
    for copy in copies:
        copy.start()
    stacked, opposite = piece_refs[:4], piece_refs[4:]
    for k in range(many):
        element = near[pos[1], k]
        dy = ((element >> 2) - pos[2]) & 3
        dz = ((element & 3) - pos[3]) & 3
        for z in range(4):
            for y in range(4):
                piece = opposite[y].at[0] if z == 2 else stacked[y].at[(0, 1, 0, 2)[z]]

                @pl.when((dz == z) & (dy == y))
                def _():
                    pltpu.make_async_copy(piece, near_coeffs.at[k], near_sem.at[k]).start()

    for copy in copies:
        copy.wait()
    for k in range(many):
        pltpu.make_async_copy(piece_refs[0].at[0], near_coeffs.at[k], near_sem.at[k]).wait()
        x = masked_copy(near_coeffs[k], counts[near[pos[1], k]])
        part = jnp.dot(hops[k].reshape(-1, width), x, preferred_element_type=jnp.float32)
        if k == 0:
            o_ref[...] = part
        else:
            o_ref[...] += part


def hop_apply(pos, counts, near, hops, pieces):
    _, many, rows, width = hops[0].shape
    blocks = len(hops)
    bands = pieces[0].shape[2]
    smem = pl.BlockSpec(memory_space=pltpu.SMEM)
    return pl.pallas_call(
        hop_kernel,
        out_shape=jax.ShapeDtypeStruct((blocks * rows, bands), jnp.float32),
        in_specs=[smem] * 3 + [pl.BlockSpec(memory_space=pltpu.HBM)] * (len(hops) + len(pieces)),
        scratch_shapes=[
            pltpu.VMEM((many, blocks, rows, width), jnp.bfloat16),
            pltpu.VMEM((many, width, bands), jnp.bfloat16),
            pltpu.SemaphoreType.DMA((blocks,)),
            pltpu.SemaphoreType.DMA((many,)),
        ],
        compiler_params=pltpu.CompilerParams(vmem_limit_bytes=60 << 20),
        cost_estimate=pl.CostEstimate(
            flops=2 * len(hops) * hops[0].size * bands,
            bytes_accessed=2 * len(hops) * hops[0].size + 2 * many * width * bands,
            transcendentals=0,
        ),
        name="hop_apply",
    )(pos, counts, near, *hops, *pieces)


def own_kernel(pos, counts, mine_ref, other_ref, x_ref, h_ref, o_ref, low):
    chips, blocks, rows, size = mine_ref.shape
    half = size // CORES
    for ref, core in ((mine_ref, pos[0]), (other_ref, 1 - pos[0])):
        at = pl.multiple_of(core * half, half)
        for g in range(chips):
            low[:, pl.ds(at + g * rows, rows), :] = ref[g]
    count = counts[pos[1]]
    x = masked_copy(x_ref[0], count)
    o_ref[...] = h_ref[...]
    for j, first in enumerate(triangle(SIDE)):
        column = low[pl.ds(first, j + 1)].reshape((j + 1) * size, size)
        here = pl.ds(j * size, size)
        o_ref[pl.ds(0, (j + 1) * size), :] += jnp.dot(
            column, x[j * size : (j + 1) * size], preferred_element_type=jnp.float32
        )
        if j:
            o_ref[here, :] += lax.dot_general(
                column[: j * size],
                x[: j * size],
                (((0,), (0,)), ((), ())),
                preferred_element_type=jnp.float32,
            )
    at = lax.broadcasted_iota(jnp.int32, o_ref.shape, 0)
    o_ref[...] = jnp.where(at < count, o_ref[...], jnp.zeros_like(o_ref))


def own_apply(pos, counts, mine, other, coeffs, hopped):
    chips, blocks, rows, size = mine.shape
    smem, vmem = pl.BlockSpec(memory_space=pltpu.SMEM), pl.BlockSpec(memory_space=pltpu.VMEM)
    return pl.pallas_call(
        own_kernel,
        out_shape=jax.ShapeDtypeStruct(hopped.shape, jnp.float32),
        in_specs=[smem, smem] + [vmem] * 4,
        scratch_shapes=[pltpu.VMEM((blocks, size, size), jnp.bfloat16)],
        compiler_params=pltpu.CompilerParams(vmem_limit_bytes=40 << 20),
        cost_estimate=pl.CostEstimate(
            flops=2 * coeffs.shape[1] ** 2 * coeffs.shape[2],
            bytes_accessed=4 * mine.size + 2 * coeffs.size + 8 * hopped.size,
            transcendentals=0,
        ),
        name="own_apply",
    )(pos, counts, mine, other, coeffs, hopped)


def local(basis_values, basis_derivs, potential, hop_blocks, coeffs, counts, neighbours):
    pos = [lax.axis_index(n) for n in ("c", ELEM, "y", "zh", "zl", "x")]
    pos = jnp.stack(pos).astype(jnp.int32)
    basis_values, pos = lax.optimization_barrier((basis_values, pos))

    def exchange(a):
        return lax.all_to_all(a, GRP, 0, 0, tiled=True)

    barrier = lax.optimization_barrier
    pair = shift(hop_blocks, "zl", 1)
    own_x = [shift(hop_blocks, "x", 1), shift(hop_blocks, "x", 3)]
    values, ring = barrier((split_points(basis_values[0]), coeffs))
    after, before = shift(ring, "zh", 1), shift(ring, "zh", 3)
    pair_x = [shift(pair, "x", 1), shift(pair, "x", 3)]
    own_far = far(*own_x, "x")
    values, after, before, pair_x, own_far = barrier(
        (values, after, before, pair_x, own_far)
    )

    values = exchange(values)
    stacked = jnp.concatenate([coeffs, after, before])
    opposite = far(after, before, "zh")
    near_y = [shift(stacked, "y", 1), shift(stacked, "y", 3)]
    pair_far = far(*pair_x, "x")
    derivs, opposite, near_y, pair_far = barrier(
        (split_points(basis_derivs[0]), opposite, near_y, pair_far)
    )

    derivs = exchange(derivs)
    width = coeffs.shape[1]
    part = value_part(potential, values.reshape(width, -1))
    part, opposite, near_y = barrier((part, opposite, near_y))
    far_y = far(*near_y, "y")
    near_o = [shift(opposite, "y", 1), shift(opposite, "y", 3)]
    pieces = [stacked, near_y[0], far_y, near_y[1]]
    pieces += [opposite, near_o[0], far(*near_o, "y"), near_o[1]]
    hops = [hop_blocks, pair, own_x[0], pair_x[0], own_x[1], pair_x[1], own_far, pair_far]
    others = [swap_cores(h) for h in hops]
    hopped = hop_apply(pos, counts, neighbours, hops + others, pieces)
    derivs, hopped, part = barrier((derivs, hopped, part))

    keep, send = deriv_part(pos, derivs.reshape(width, -1), part)
    part = (keep + swap_cores(send)).astype(jnp.bfloat16)
    part = lax.all_to_all(part, CHIPS, 0, 0, tiled=True).astype(jnp.float32)
    part = part.sum(0).astype(jnp.bfloat16)
    chips = lax.axis_size(CHIPS)
    low = jnp.broadcast_to(part[None], (chips, *part.shape))
    low = lax.all_to_all(low, CHIPS, 0, 0, tiled=True)
    result = own_apply(pos, counts, low, swap_cores(low), coeffs, hopped)
    return result[None]


def solution(mesh):
    fine = Mesh(mesh.devices.reshape(4, 4, 2, 4, 2), ("y", "zh", "zl", "x", "c"))
    placed = (
        P(ELEM, GRP, None),
        P(ELEM, GRP, None),
        P(ELEM, GRP),
        P(ELEM, None, GRP, None),
        P(ELEM, None, GRP),
        P(),
        P(),
    )
    return jax.shard_map(
        local, mesh=fine, in_specs=placed, out_specs=P(ELEM, None, GRP), check_vma=False
    )
```
